32 devices in a mesh: frame: 8 (over y, x, core), chan: 4 (over z).
Axes of the slice: x: 2, y: 2, z: 4, core: 2. Of those that a mesh axis runs over, the one named last changes fastest.
Arguments:
- latent: bfloat16 [8, 512, 2560], P('frame', 'chan'), may hold values from -6 to 6
- spatial_w: bfloat16 [512, 4608], P('chan'), may hold values from -0.09375 to 0.09375
- spatial_b: float32 [512], P('chan'), may hold values from -0.5 to 0.5
- temporal_w: float32 [3, 512], P(None, 'chan'), may hold values from -3 to 3
- temporal_b: float32 [512], P('chan'), may hold values from -1 to 1
Outputs:
- decoded: bfloat16 [8, 512, 2560], P('frame', 'chan')
The draws below stay inside these ranges and needn't reach their ends.
All inputs are finite; a program needn't handle non-finite values.
Results may differ from the reference program's by a relative error of at most 0.0048.
Values may be sent and summed in bfloat16 or wider, within the bound.
No kernel may reach another device: no remote copies, remote signals or barrier semaphores. Data moves between devices by JAX's collectives and lax.ppermute only.
A program may use at most 64 MiB of HBM per device.

```python
import jax
import jax.numpy as jnp
from jax import lax

C = 512
W = 160
FRAMES = 8
H = 16


def level_of(rng, dims, pieces, low, high):
    def one(position, blocks):
        steps = jax.random.uniform(jax.random.fold_in(jax.random.fold_in(rng, 6), position), (blocks,), jnp.float32, low / len(pieces), high / len(pieces))
        return jnp.repeat(jnp.exp(steps), dims[position] // blocks).reshape((-1,) + (1,) * (len(dims) - position - 1))

    level = one(*pieces[0])
    for cut in pieces[1:]:
        level = level * one(*cut)
    return level


def noise(key, dims, width, reach, pieces=(), kind=jnp.bfloat16):
    array = jax.random.normal(key, dims, jnp.float32) * width
    if len(pieces) > 0:
        array = level_of(key, dims, pieces, -0.22, 0.18) * array
    return jnp.clip(array, min=-reach, max=reach).astype(kind)


def setup_inputs(seed: int = 0) -> dict:
    seeds = jax.random.split(jax.random.key(seed), 6)
    return {
        "latent": noise(seeds[0], (FRAMES, C, H * W), 1.0, 6.0, ((0, 8), (1, 4))),
        "spatial_w": noise(seeds[1], (C, 9 * C), (9 * C) ** -0.5, 0.09375, ((0, 4),)),
        "spatial_b": jnp.clip(jax.random.uniform(seeds[2], (C,), jnp.float32, -0.5, 0.5) * level_of(seeds[2], (C,), ((0, 4),), -0.4, 0.0), -0.5, 0.5),
        "temporal_w": noise(seeds[3], (3, C), 0.6, 3.0, ((1, 4),), jnp.float32),
        "temporal_b": jnp.clip(jax.random.uniform(seeds[4], (C,), jnp.float32, -1.0, 1.0) * level_of(seeds[4], (C,), ((0, 4),), -0.4, 0.0), -1.0, 1.0),
    }


def reference(latent, spatial_w, spatial_b, temporal_w, temporal_b):
    frames = latent.shape[0]
    chans = latent.shape[1]
    image = latent.astype(jnp.float32).reshape(frames, chans, H, W)
    filters = spatial_w.astype(jnp.float32).reshape(chans, 3, 3, chans).transpose(0, 3, 1, 2)
    spatial = lax.conv_general_dilated(image, filters, (1, 1), ((1, 1), (1, 1)), dimension_numbers=("NCHW", "OIHW", "NCHW"), precision=lax.Precision.HIGHEST)
    spatial = (spatial + spatial_b[None, :, None, None]).astype(jnp.bfloat16)
    values = spatial.astype(jnp.float32).reshape(frames, chans, H * W)
    padded = jnp.pad(values, ((2, 0), (0, 0), (0, 0)))
    taps = temporal_w[:, None, :, None]
    total = temporal_b[None, :, None] + taps[0] * padded[0:frames] + taps[1] * padded[1:frames + 1] + taps[2] * padded[2:frames + 2]
    return total.astype(jnp.bfloat16)
```

```python
import jax
import jax.numpy as jnp
from jax import lax
from jax.sharding import PartitionSpec as P

W = 160
CUT = 12


def convolve(image, filters, padding):
    return lax.conv_general_dilated(
        image,
        filters,
        (1, 1),
        padding,
        dimension_numbers=("NCHW", "OIHW", "NCHW"),
        preferred_element_type=jnp.float32,
    )


def three_taps(history, values, temporal_w, temporal_b):
    joined = jnp.concatenate([history, values], axis=0).astype(jnp.float32)
    frames = values.shape[0]
    extra = (1,) * (values.ndim - 2)
    taps = temporal_w.reshape((3, 1, temporal_w.shape[1]) + extra)
    bias = temporal_b.reshape((1, temporal_b.shape[0]) + extra)
    total = (
        bias
        + taps[0] * joined[0:frames]
        + taps[1] * joined[1 : frames + 1]
        + taps[2] * joined[2 : frames + 2]
    )
    return total.astype(jnp.bfloat16)


def gathered(latent, spatial_w, spatial_b, temporal_w, temporal_b):
    frames, local_chan, pixels = latent.shape
    rows = pixels // W
    full_chan = spatial_w.shape[1] // 9
    shaped_w = spatial_w.reshape(spatial_w.shape[0], 3, 3, full_chan)
    piece = lax.all_gather(latent, "chan", axis=1, tiled=True)
    image = piece.reshape(frames, full_chan, rows, W)
    summed = convolve(image, shaped_w.transpose(0, 3, 1, 2), ((1, 1), (1, 1)))
    summed = summed.reshape(frames, spatial_w.shape[0], pixels)
    spatial = (summed + spatial_b[None, :, None]).astype(jnp.bfloat16)
    band_count = lax.axis_size("frame")
    banded = spatial.reshape(frames, local_chan, band_count, pixels // band_count)
    band = lax.all_to_all(banded, "frame", split_axis=2, concat_axis=0, tiled=True)
    zeros = jnp.zeros((2,) + band.shape[1:], jnp.bfloat16)
    filtered = three_taps(zeros, band, temporal_w, temporal_b)
    result = lax.all_to_all(filtered, "frame", split_axis=0, concat_axis=2, tiled=True)
    return result.reshape(frames, local_chan, pixels)


def relayed(latent, spatial_w, spatial_b, temporal_w, temporal_b):
    _, local_chan, pixels = latent.shape
    out_chan = spatial_w.shape[0]
    rows = pixels // W
    frame_count = lax.axis_size("frame")
    chan_count = lax.axis_size("chan")
    chan = lax.axis_index("chan")
    odd = lax.axis_index("frame") % 2
    pair = [(f, f ^ 1) for f in range(frame_count)]
    hop = []
    for f in range(frame_count):
        for z in range(chan_count):
            to = z + 1 - 2 * (f % 2)
            if 0 <= to < chan_count:
                hop.append((f * chan_count + z, f * chan_count + to))

    def swap(x):
        return lax.ppermute(x, "frame", pair)

    def relay(x):
        return lax.ppermute(x, ("frame", "chan"), hop)

    step = 1 - 2 * odd
    order = [chan, (chan - step) % chan_count, (chan + step) % chan_count, (chan + 2) % chan_count]
    shaped_w = spatial_w.reshape(out_chan, 9, chan_count, local_chan)
    filters = jnp.concatenate(
        [lax.dynamic_index_in_dim(shaped_w, block, 2, keepdims=False) for block in order], axis=2
    )
    filters = filters.reshape(out_chan, 3, 3, chan_count * local_chan).transpose(0, 3, 1, 2)

    partner = swap(latent)
    bounds = [(0, CUT), (CUT, rows)]
    both = [
        jnp.concatenate([latent[:, :, a * W : b * W], partner[:, :, a * W : b * W]], axis=0)
        for a, b in bounds
    ]
    hops = [[], []]
    for r in range(3):
        for k in range(2):
            hops[k].append(relay(hops[k][-1] if r else both[k]))
    images = []
    for k, (a, b) in enumerate(bounds):
        straight = [h[0:1] for h in hops[k]]
        crossed = [swap(h[1:2]) for h in hops[k]]
        parts = [
            latent[:, :, a * W : b * W],
            straight[0] + crossed[2],
            crossed[0] + straight[2],
            straight[1] + crossed[1],
        ]
        images.append(jnp.concatenate(parts, axis=1).reshape(1, chan_count * local_chan, b - a, W))

    def finish(image, padding):
        summed = convolve(image, filters, padding)
        summed = summed.reshape(1, out_chan, summed.shape[2] * W)
        spatial = (summed + spatial_b[None, :, None]).astype(jnp.bfloat16)
        second = lax.ppermute(spatial, "frame", [(f, f + 2) for f in range(frame_count - 2)])
        first = swap(jnp.where(odd == 0, spatial, second))
        return three_taps(jnp.concatenate([second, first], axis=0), spatial, temporal_w, temporal_b)

    top = finish(images[0], ((1, 0), (1, 1)))
    low = jnp.concatenate([images[0][:, :, CUT - 2 :], images[1]], axis=2)
    bottom = finish(low, ((0, 1), (1, 1)))
    return jnp.concatenate([top, bottom], axis=2)


def shards(latent, *rest):
    if lax.axis_size("chan") == 4 and lax.axis_size("frame") % 2 == 0 and latent.shape[0] == 1:
        return relayed(latent, *rest)
    return gathered(latent, *rest)


def solution(mesh):
    placed = (P("frame", "chan", None), P("chan", None), P("chan"), P(None, "chan"), P("chan"))
    return jax.shard_map(
        shards, mesh=mesh, in_specs=placed, out_specs=P("frame", "chan", None), check_vma=False
    )
```

```python
import functools

import jax
import jax.numpy as jnp
from jax import lax
from jax.experimental import pallas as pl
from jax.experimental.pallas import tpu as pltpu
from jax.sharding import PartitionSpec as P


W = 160
CUTS = (8, 12)


VMEM = pl.BlockSpec(memory_space=pltpu.VMEM)
ANY = pl.BlockSpec(memory_space=pl.ANY)


def three_taps(history, values, temporal_w, temporal_b):
    joined = jnp.concatenate([history, values], axis=0).astype(jnp.float32)
    frames = values.shape[0]
    extra = (1,) * (values.ndim - 2)
    taps = temporal_w.reshape((3, 1, temporal_w.shape[1]) + extra)
    bias = temporal_b.reshape((1, temporal_b.shape[0]) + extra)
    total = (
        bias
        + taps[0] * joined[0:frames]
        + taps[1] * joined[1 : frames + 1]
        + taps[2] * joined[2 : frames + 2]
    )
    return total.astype(jnp.bfloat16)


def gathered(latent, spatial_w, spatial_b, temporal_w, temporal_b):
    frames, local_chan, pixels = latent.shape
    rows = pixels // W
    full_chan = spatial_w.shape[1] // 9
    shaped_w = spatial_w.reshape(spatial_w.shape[0], 3, 3, full_chan)
    piece = lax.all_gather(latent, "chan", axis=1, tiled=True)
    image = piece.reshape(frames, full_chan, rows, W)
    summed = lax.conv_general_dilated(
        image,
        shaped_w.transpose(0, 3, 1, 2),
        (1, 1),
        ((1, 1), (1, 1)),
        dimension_numbers=("NCHW", "OIHW", "NCHW"),
        preferred_element_type=jnp.float32,
    )
    summed = summed.reshape(frames, spatial_w.shape[0], pixels)
    spatial = (summed + spatial_b[None, :, None]).astype(jnp.bfloat16)
    band_count = lax.axis_size("frame")
    banded = spatial.reshape(frames, local_chan, band_count, pixels // band_count)
    band = lax.all_to_all(banded, "frame", split_axis=2, concat_axis=0, tiled=True)
    zeros = jnp.zeros((2,) + band.shape[1:], jnp.bfloat16)
    filtered = three_taps(zeros, band, temporal_w, temporal_b)
    result = lax.all_to_all(filtered, "frame", split_axis=0, concat_axis=2, tiled=True)
    return result.reshape(frames, local_chan, pixels)


def place():
    group, frame = lax.axis_index("chan"), lax.axis_index("frame")
    return group, frame, frame & 1, (frame & 1) == (group & 1), (frame >> 1) & 1


def copies(pairs, sems):
    moves = [pltpu.make_async_copy(a, b, sems.at[n]) for n, (a, b) in enumerate(pairs)]
    for move in moves:
        move.start()
    return moves


def split_kernel(latent_ref, w_ref, b_ref, half_ref, *refs, starts, stops):
    own_refs, (frame_ref, sems) = refs[:-2], refs[-2:]
    side = place()[4]
    half, width = half_ref.shape[0], w_ref.shape[1]
    outs = w_ref.shape[0]
    first = pl.multiple_of(side * half, half)
    moves = copies(
        [
            (w_ref.at[pl.ds(first, half), :], half_ref.at[:, 0:width]),
            (latent_ref.at[0], frame_ref),
        ],
        sems,
    )
    bias = b_ref[...]
    high = bias.astype(jnp.bfloat16)
    rest = bias - high.astype(jnp.float32)
    middle = rest.astype(jnp.bfloat16)
    low = (rest - middle.astype(jnp.float32)).astype(jnp.bfloat16)
    row = lax.broadcasted_iota(jnp.int32, (outs, outs), 0)
    pieces = jnp.where(
        row == 0,
        high.astype(jnp.float32),
        jnp.where(
            row == 1,
            middle.astype(jnp.float32),
            jnp.where(row == 2, low.astype(jnp.float32), 0.0),
        ),
    ).T
    half_ref[:, width:] = jnp.where(side == 0, pieces[0:half], pieces[half:]).astype(jnp.bfloat16)
    moves[1].wait()
    for own_ref, a, b in zip(own_refs, starts, stops):
        own_ref[...] = frame_ref[:, a * W : b * W].T
    moves[0].wait()


def order_kernel(w_ref, b_ref, mine_ref, other_ref, out_ref, bias_ref, rows_ref, sems):
    outs, width = w_ref.shape
    chans = out_ref.shape[1] // 4
    half = outs // 2
    group, _, _, straight, side = place()
    one, two, three = group ^ 1, group ^ 2, group ^ 3
    order = [
        jnp.where(straight, two, one),
        jnp.where(straight, one, two),
        jnp.where(straight, three, group),
        jnp.where(straight, group, three),
    ]

    @pl.when(jnp.logical_not(straight))
    def _():
        for move in copies([(w_ref, rows_ref.at[:, 0:width])], sems):
            move.wait()
        bias_ref[...] = b_ref[...]

    @pl.when(straight)
    def _():
        here = pl.multiple_of(side * half, half)
        there = pl.multiple_of((1 - side) * half, half)
        pairs = [
            (mine_ref, rows_ref.at[pl.ds(here, half), :]),
            (other_ref, rows_ref.at[pl.ds(there, half), :]),
        ]
        for move in copies(pairs, sems):
            move.wait()
        pieces = rows_ref[:, width:].astype(jnp.float32).T
        bias_ref[...] = pieces[0:1] + pieces[1:2] + pieces[2:3]

    for slot in range(4):
        for i in range(3):
            for j in range(3):
                start = pl.multiple_of(((i * 3 + j) * 4 + order[slot]) * chans, chans)
                tile = rows_ref[:, pl.ds(start, chans)]
                out_ref[i, slot * chans : (slot + 1) * chans, j * outs : (j + 1) * outs] = tile.T


def conv_kernel(
    first_ref, crossed_ref, second_ref, own_ref, passed_ref, above_ref, w_ref, b_ref,
    out_ref, tail_ref, x_ref, sems, *, top, low
):
    size, outs = out_ref.shape
    pixels, chans = own_ref.shape
    above = W if top else 2 * W
    straight = place()[3]
    body = slice(above, above + pixels)
    moves = copies(
        [
            (first_ref, x_ref.at[body, 0:chans]),
            (crossed_ref, x_ref.at[body, chans : 2 * chans]),
            (second_ref, x_ref.at[body, 2 * chans : 3 * chans]),
        ],
        sems,
    )
    last = x_ref.at[body, 3 * chans :]

    @pl.when(straight)
    def _():
        pltpu.make_async_copy(own_ref, last, sems.at[3]).start()

    @pl.when(jnp.logical_not(straight))
    def _():
        pltpu.make_async_copy(passed_ref, last, sems.at[3]).start()

    x_ref[0:above, :] = jnp.zeros((W, 4 * chans), x_ref.dtype) if top else above_ref[...]
    if low:
        x_ref[above + pixels :, :] = jnp.zeros((W, 4 * chans), x_ref.dtype)
    for move in moves:
        move.wait()
    pltpu.make_async_copy(own_ref, last, sems.at[3]).wait()
    if not low:
        tail_ref[...] = x_ref[above + pixels - 2 * W : above + pixels, :]
    total = jnp.dot(x_ref[0:size, :], w_ref[0], preferred_element_type=jnp.float32)
    for i in range(1, 3):
        total += jnp.dot(
            x_ref[i * W : i * W + size, :], w_ref[i], preferred_element_type=jnp.float32
        )
    column = lax.broadcasted_iota(jnp.int32, (size, outs), 0) % W
    left = jnp.where(column == 0, 0.0, pltpu.roll(total[:, 0:outs], 1, 0))
    right = jnp.where(column == W - 1, 0.0, pltpu.roll(total[:, 2 * outs :], size - 1, 0))
    out_ref[...] = (left + total[:, outs : 2 * outs] + right + b_ref[...]).astype(out_ref.dtype)


def taps_kernel(values_ref, before_ref, previous_ref, taps_ref, bias_ref, *refs):
    out_ref = refs[-1]
    frame = place()[1]
    before = jnp.where(frame >= 2, before_ref[...].astype(jnp.float32), 0.0)
    previous = jnp.where(frame >= 1, previous_ref[...].astype(jnp.float32), 0.0)
    total = (
        bias_ref[...]
        + taps_ref[0:1, :] * before
        + taps_ref[1:2, :] * previous
        + taps_ref[2:3, :] * values_ref[...].astype(jnp.float32)
    )
    out_ref[...] = total.astype(out_ref.dtype).T


def limit(mib):
    return pltpu.CompilerParams(vmem_limit_bytes=mib << 20)


def split_work(latent, spatial_w, spatial_b, temporal_w, temporal_b):
    _, local_chan, pixels = latent.shape
    outs, width = spatial_w.shape
    rows = pixels // W
    frame_count = lax.axis_size("frame")
    core = lax.axis_index("frame") & 1
    both = ("frame", "chan")

    def table(rule):
        moves = []
        for f in range(frame_count):
            for z in range(4):
                to_z, to_c = rule(z, f % 2)
                moves.append((f * 4 + z, (f - f % 2 + to_c) * 4 + to_z))
        return moves

    near = table(lambda z, c: (z ^ 2, c) if z % 2 == c else (z ^ 1, 1 - c))
    far = table(lambda z, c: (z, 1 - c) if z % 2 == c else (z ^ 3, c))
    home = table(lambda z, c: (z - z % 2 + 1 - c, z % 2))
    out = [(b, a) for a, b in home]
    ahead = [(a, (b + 8) % (4 * frame_count)) for a, b in home]
    pair = [(f, f ^ 1) for f in range(frame_count)]
    across = []
    for f in range(frame_count):
        for z in range(4):
            across.append((f * 4 + z, (f ^ 2 if z % 2 == f % 2 else f) * 4 + z))

    def swap(x):
        return lax.ppermute(x, "frame", pair)

    cuts = [c for c in CUTS if c < rows - 1]
    starts = [0] + [c + 1 for c in cuts]
    stops = [c + 1 for c in cuts] + [rows]
    bias_row = spatial_b.reshape(1, outs)
    mine, *owns = pl.pallas_call(
        functools.partial(split_kernel, starts=starts, stops=stops),
        out_shape=[jax.ShapeDtypeStruct((outs // 2, width + 128), jnp.bfloat16)]
        + [
            jax.ShapeDtypeStruct(((b - a) * W, local_chan), jnp.bfloat16)
            for a, b in zip(starts, stops)
        ],
        in_specs=[ANY, ANY, VMEM],
        out_specs=[VMEM] * (1 + len(starts)),
        scratch_shapes=[
            pltpu.VMEM((local_chan, pixels), jnp.bfloat16),
            pltpu.SemaphoreType.DMA((2,)),
        ],
        compiler_params=limit(8),
        name="split",
    )(latent, spatial_w, bias_row)

    mine = lax.ppermute(mine, both, out)
    other = lax.ppermute(mine, both, across)
    filters, bias = pl.pallas_call(
        order_kernel,
        out_shape=(
            jax.ShapeDtypeStruct((3, 4 * local_chan, 3 * outs), jnp.bfloat16),
            jax.ShapeDtypeStruct((1, outs), jnp.float32),
        ),
        in_specs=[ANY, VMEM, ANY, ANY],
        out_specs=(VMEM, VMEM),
        scratch_shapes=[
            pltpu.VMEM((outs, width + 128), jnp.bfloat16),
            pltpu.SemaphoreType.DMA((2,)),
        ],
        compiler_params=limit(8),
        name="order",
    )(spatial_w, bias_row, mine, other)

    arrived = []
    for own in owns:
        first = lax.ppermute(own, both, near)
        second = lax.ppermute(own, both, far)
        arrived.append((own, first, second))

    decoded, tail, column = None, jnp.zeros((2 * W, 4 * local_chan), jnp.bfloat16), 0
    for k, (own, first, second) in enumerate(arrived):
        crossed = swap(first)
        passed = swap(second)
        low = k == len(arrived) - 1
        size = own.shape[0] - W * (k == 0) + W * low
        done, tail = pl.pallas_call(
            functools.partial(conv_kernel, top=k == 0, low=low),
            out_shape=(
                jax.ShapeDtypeStruct((size, outs), jnp.bfloat16),
                jax.ShapeDtypeStruct((2 * W, 4 * local_chan), jnp.bfloat16),
            ),
            in_specs=[ANY] * 5 + [VMEM] * 3,
            out_specs=(VMEM, VMEM),
            scratch_shapes=[
                pltpu.VMEM((size + 2 * W, 4 * local_chan), jnp.bfloat16),
                pltpu.SemaphoreType.DMA((4,)),
            ],
            compiler_params=limit(20),
            name="conv",
        )(first, crossed, second, own, passed, tail, filters, bias)
        spatial = lax.ppermute(done, both, home)
        before = lax.ppermute(done, both, ahead)
        previous = swap(jnp.where(core == 1, before, spatial))
        held = [] if decoded is None else [decoded]
        block = column // size
        decoded = pl.pallas_call(
            taps_kernel,
            out_shape=jax.ShapeDtypeStruct((outs, pixels), jnp.bfloat16),
            grid=(1,),
            in_specs=[VMEM] * 5 + [ANY] * len(held),
            out_specs=pl.BlockSpec((outs, size), lambda n, block=block: (0, block)),
            input_output_aliases={5: 0} if held else {},
            compiler_params=limit(8),
            name="taps",
        )(spatial, before, previous, temporal_w, temporal_b.reshape(1, outs), *held)
        column += size
    return decoded[None]


def shards(latent, *rest):
    if lax.axis_size("chan") == 4 and lax.axis_size("frame") % 4 == 0 and latent.shape[0] == 1:
        return split_work(latent, *rest)
    return gathered(latent, *rest)


def solution(mesh):
    placed = (P("frame", "chan", None), P("chan", None), P("chan"), P(None, "chan"), P("chan"))
    return jax.shard_map(
        shards, mesh=mesh, in_specs=placed, out_specs=P("frame", "chan", None), check_vma=False
    )
```

```python
import functools

import jax
import jax.numpy as jnp
from jax import lax
from jax.experimental import pallas as pl
from jax.experimental.pallas import tpu as pltpu
from jax.sharding import PartitionSpec as P


W = 160
CUTS = (8, 12)


VMEM = pl.BlockSpec(memory_space=pltpu.VMEM)
ANY = pl.BlockSpec(memory_space=pl.ANY)
HBM = pl.BlockSpec(memory_space=pltpu.HBM)


def three_taps(history, values, temporal_w, temporal_b):
    joined = jnp.concatenate([history, values], axis=0).astype(jnp.float32)
    frames = values.shape[0]
    extra = (1,) * (values.ndim - 2)
    taps = temporal_w.reshape((3, 1, temporal_w.shape[1]) + extra)
    bias = temporal_b.reshape((1, temporal_b.shape[0]) + extra)
    total = (
        bias
        + taps[0] * joined[0:frames]
        + taps[1] * joined[1 : frames + 1]
        + taps[2] * joined[2 : frames + 2]
    )
    return total.astype(jnp.bfloat16)


def gathered(latent, spatial_w, spatial_b, temporal_w, temporal_b):
    frames, local_chan, pixels = latent.shape
    rows = pixels // W
    full_chan = spatial_w.shape[1] // 9
    shaped_w = spatial_w.reshape(spatial_w.shape[0], 3, 3, full_chan)
    piece = lax.all_gather(latent, "chan", axis=1, tiled=True)
    image = piece.reshape(frames, full_chan, rows, W)
    summed = lax.conv_general_dilated(
        image,
        shaped_w.transpose(0, 3, 1, 2),
        (1, 1),
        ((1, 1), (1, 1)),
        dimension_numbers=("NCHW", "OIHW", "NCHW"),
        preferred_element_type=jnp.float32,
    )
    summed = summed.reshape(frames, spatial_w.shape[0], pixels)
    spatial = (summed + spatial_b[None, :, None]).astype(jnp.bfloat16)
    band_count = lax.axis_size("frame")
    banded = spatial.reshape(frames, local_chan, band_count, pixels // band_count)
    band = lax.all_to_all(banded, "frame", split_axis=2, concat_axis=0, tiled=True)
    zeros = jnp.zeros((2,) + band.shape[1:], jnp.bfloat16)
    filtered = three_taps(zeros, band, temporal_w, temporal_b)
    result = lax.all_to_all(filtered, "frame", split_axis=0, concat_axis=2, tiled=True)
    return result.reshape(frames, local_chan, pixels)


def place():
    group, frame = lax.axis_index("chan"), lax.axis_index("frame")
    return group, frame, frame & 1, (frame & 1) == (group & 1), (frame >> 1) & 1


def copies(pairs, sems):
    moves = [pltpu.make_async_copy(a, b, sems.at[n]) for n, (a, b) in enumerate(pairs)]
    for move in moves:
        move.start()
    return moves


def split_kernel(latent_ref, w_ref, b_ref, half_ref, *refs, starts, stops):
    own_refs, (frame_ref, bias_ref, sems) = refs[:-3], refs[-3:]
    side = place()[4]
    half, width = half_ref.shape[0], w_ref.shape[1]
    outs = w_ref.shape[0]
    first = pl.multiple_of(side * half, half)
    moves = copies(
        [
            (w_ref.at[pl.ds(first, half), :], half_ref.at[:, 0:width]),
            (latent_ref.at[0], frame_ref),
            (b_ref, bias_ref),
        ],
        sems,
    )
    moves[1].wait()
    for own_ref, a, b in zip(own_refs, starts, stops):
        own_ref[...] = frame_ref[:, a * W : b * W].T
    moves[2].wait()
    bias = bias_ref[...]
    high = bias.astype(jnp.bfloat16)
    rest = bias - high.astype(jnp.float32)
    middle = rest.astype(jnp.bfloat16)
    low = (rest - middle.astype(jnp.float32)).astype(jnp.bfloat16)
    row = lax.broadcasted_iota(jnp.int32, (outs, outs), 0)
    pieces = jnp.where(
        row == 0,
        high.astype(jnp.float32),
        jnp.where(
            row == 1,
            middle.astype(jnp.float32),
            jnp.where(row == 2, low.astype(jnp.float32), 0.0),
        ),
    ).T
    half_ref[:, width:] = jnp.where(side == 0, pieces[0:half], pieces[half:]).astype(jnp.bfloat16)
    moves[0].wait()


def order_kernel(w_ref, b_ref, mine_ref, other_ref, out_ref, bias_ref, rows_ref, sems):
    outs, width = w_ref.shape
    chans = out_ref.shape[1] // 4
    half = outs // 2
    group, _, _, straight, side = place()
    one, two, three = group ^ 1, group ^ 2, group ^ 3
    order = [
        jnp.where(straight, two, one),
        jnp.where(straight, one, two),
        jnp.where(straight, three, group),
        jnp.where(straight, group, three),
    ]

    @pl.when(jnp.logical_not(straight))
    def _():
        for move in copies([(w_ref, rows_ref.at[:, 0:width]), (b_ref, bias_ref)], sems):
            move.wait()

    @pl.when(straight)
    def _():
        here = pl.multiple_of(side * half, half)
        there = pl.multiple_of((1 - side) * half, half)
        pairs = [
            (mine_ref, rows_ref.at[pl.ds(here, half), :]),
            (other_ref, rows_ref.at[pl.ds(there, half), :]),
        ]
        for move in copies(pairs, sems):
            move.wait()
        pieces = rows_ref[:, width:].astype(jnp.float32).T
        bias_ref[...] = pieces[0:1] + pieces[1:2] + pieces[2:3]

    for slot in range(4):
        for i in range(3):
            for j in range(3):
                start = pl.multiple_of(((i * 3 + j) * 4 + order[slot]) * chans, chans)
                tile = rows_ref[:, pl.ds(start, chans)]
                out_ref[i, slot * chans : (slot + 1) * chans, j * outs : (j + 1) * outs] = tile.T


def conv_kernel(
    first_ref, crossed_ref, second_ref, own_ref, passed_ref, above_ref, w_ref, b_ref,
    out_ref, tail_ref, x_ref, sems, *, top, low
):
    size, outs = out_ref.shape
    pixels, chans = own_ref.shape
    above = W if top else 2 * W
    straight = place()[3]
    body = slice(above, above + pixels)
    moves = copies(
        [
            (first_ref, x_ref.at[body, 0:chans]),
            (crossed_ref, x_ref.at[body, chans : 2 * chans]),
            (second_ref, x_ref.at[body, 2 * chans : 3 * chans]),
        ],
        sems,
    )
    last = x_ref.at[body, 3 * chans :]

    @pl.when(straight)
    def _():
        pltpu.make_async_copy(own_ref, last, sems.at[3]).start()

    @pl.when(jnp.logical_not(straight))
    def _():
        pltpu.make_async_copy(passed_ref, last, sems.at[3]).start()

    x_ref[0:above, :] = jnp.zeros((W, 4 * chans), x_ref.dtype) if top else above_ref[...]
    if low:
        x_ref[above + pixels :, :] = jnp.zeros((W, 4 * chans), x_ref.dtype)
    for move in moves:
        move.wait()
    pltpu.make_async_copy(own_ref, last, sems.at[3]).wait()
    if not low:
        tail_ref[...] = x_ref[above + pixels - 2 * W : above + pixels, :]
    total = jnp.dot(x_ref[0:size, :], w_ref[0], preferred_element_type=jnp.float32)
    for i in range(1, 3):
        total += jnp.dot(
            x_ref[i * W : i * W + size, :], w_ref[i], preferred_element_type=jnp.float32
        )
    column = lax.broadcasted_iota(jnp.int32, (size, outs), 0) % W
    left = jnp.where(column == 0, 0.0, pltpu.roll(total[:, 0:outs], 1, 0))
    right = jnp.where(column == W - 1, 0.0, pltpu.roll(total[:, 2 * outs :], size - 1, 0))
    out_ref[...] = (left + total[:, outs : 2 * outs] + right + b_ref[...]).astype(out_ref.dtype)


def taps_kernel(values_ref, before_ref, previous_ref, taps_ref, bias_ref, *refs, column):
    decoded_ref, out_ref, sem = refs[-3:]
    frame = place()[1]
    before = jnp.where(frame >= 2, before_ref[...].astype(jnp.float32), 0.0)
    previous = jnp.where(frame >= 1, previous_ref[...].astype(jnp.float32), 0.0)
    total = (
        bias_ref[...]
        + taps_ref[0:1, :] * before
        + taps_ref[1:2, :] * previous
        + taps_ref[2:3, :] * values_ref[...].astype(jnp.float32)
    )
    out_ref[...] = total.astype(out_ref.dtype).T
    target = decoded_ref.at[:, column : column + out_ref.shape[1]]
    move = pltpu.make_async_copy(out_ref, target, sem)
    move.start()
    move.wait()


def in_hbm(x):
    return pltpu.with_memory_space_constraint(x, pltpu.HBM)


def limit(mib):
    return pltpu.CompilerParams(vmem_limit_bytes=mib << 20)


def split_work(latent, spatial_w, spatial_b, temporal_w, temporal_b):
    _, local_chan, pixels = latent.shape
    outs, width = spatial_w.shape
    rows = pixels // W
    frame_count = lax.axis_size("frame")
    core = lax.axis_index("frame") & 1
    both = ("frame", "chan")

    def table(rule):
        moves = []
        for f in range(frame_count):
            for z in range(4):
                to_z, to_c = rule(z, f % 2)
                moves.append((f * 4 + z, (f - f % 2 + to_c) * 4 + to_z))
        return moves

    near = table(lambda z, c: (z ^ 2, c) if z % 2 == c else (z ^ 1, 1 - c))
    far = table(lambda z, c: (z, 1 - c) if z % 2 == c else (z ^ 3, c))
    home = table(lambda z, c: (z - z % 2 + 1 - c, z % 2))
    out = [(b, a) for a, b in home]
    ahead = [(a, (b + 8) % (4 * frame_count)) for a, b in home]
    pair = [(f, f ^ 1) for f in range(frame_count)]
    behind = []
    for (a, b), (_, c) in zip(home, ahead):
        behind.append((a, b + 4 if b // 4 % 2 == 0 else c - 4))
    across = []
    for f in range(frame_count):
        for z in range(4):
            across.append((f * 4 + z, (f ^ 2 if z % 2 == f % 2 else f ^ 4) * 4 + z))

    def swap(x):
        return lax.ppermute(x, "frame", pair)

    cuts = [c for c in CUTS if c < rows - 1]
    starts = [0] + [c + 1 for c in cuts]
    stops = [c + 1 for c in cuts] + [rows]
    bias_row = spatial_b.reshape(1, outs)
    mine, *owns = pl.pallas_call(
        functools.partial(split_kernel, starts=starts, stops=stops),
        out_shape=[jax.ShapeDtypeStruct((outs // 2, width + 128), jnp.bfloat16)]
        + [
            jax.ShapeDtypeStruct(((b - a) * W, local_chan), jnp.bfloat16)
            for a, b in zip(starts, stops)
        ],
        in_specs=[HBM, HBM, HBM],
        out_specs=[VMEM] * (1 + len(starts)),
        scratch_shapes=[
            pltpu.VMEM((local_chan, pixels), jnp.bfloat16),
            pltpu.VMEM((1, outs), jnp.float32),
            pltpu.SemaphoreType.DMA((3,)),
        ],
        compiler_params=limit(8),
        name="split",
    )(in_hbm(latent), in_hbm(spatial_w), in_hbm(bias_row))

    mine = lax.ppermute(mine, both, out)
    other = lax.ppermute(mine, both, across)
    filters, bias = pl.pallas_call(
        order_kernel,
        out_shape=(
            jax.ShapeDtypeStruct((3, 4 * local_chan, 3 * outs), jnp.bfloat16),
            jax.ShapeDtypeStruct((1, outs), jnp.float32),
        ),
        in_specs=[HBM, HBM, ANY, ANY],
        out_specs=(VMEM, VMEM),
        scratch_shapes=[
            pltpu.VMEM((outs, width + 128), jnp.bfloat16),
            pltpu.SemaphoreType.DMA((2,)),
        ],
        compiler_params=limit(8),
        name="order",
    )(in_hbm(spatial_w), in_hbm(bias_row), mine, other)

    arrived = []
    for own in owns:
        first = lax.ppermute(own, both, near)
        second = lax.ppermute(own, both, far)
        arrived.append((own, first, second))

    decoded, tail, column = None, jnp.zeros((2 * W, 4 * local_chan), jnp.bfloat16), 0
    for k, (own, first, second) in enumerate(arrived):
        crossed = swap(first)
        passed = swap(second)
        low = k == len(arrived) - 1
        size = own.shape[0] - W * (k == 0) + W * low
        done, tail = pl.pallas_call(
            functools.partial(conv_kernel, top=k == 0, low=low),
            out_shape=(
                jax.ShapeDtypeStruct((size, outs), jnp.bfloat16),
                jax.ShapeDtypeStruct((2 * W, 4 * local_chan), jnp.bfloat16),
            ),
            in_specs=[ANY] * 5 + [VMEM] * 3,
            out_specs=(VMEM, VMEM),
            scratch_shapes=[
                pltpu.VMEM((size + 2 * W, 4 * local_chan), jnp.bfloat16),
                pltpu.SemaphoreType.DMA((4,)),
            ],
            compiler_params=limit(20),
            name="conv",
        )(first, crossed, second, own, passed, tail, filters, bias)
        spatial = lax.ppermute(done, both, home)
        before = lax.ppermute(done, both, ahead)
        if low:
            previous = lax.ppermute(done, both, behind)
        else:
            previous = swap(jnp.where(core == 1, before, spatial))
        held = [] if decoded is None else [decoded]
        decoded = pl.pallas_call(
            functools.partial(taps_kernel, column=column),
            out_shape=jax.ShapeDtypeStruct((outs, pixels), jnp.bfloat16),
            in_specs=[VMEM] * 5 + [HBM] * len(held),
            out_specs=HBM,
            scratch_shapes=[
                pltpu.VMEM((outs, size), jnp.bfloat16),
                pltpu.SemaphoreType.DMA,
            ],
            input_output_aliases={5: 0} if held else {},
            compiler_params=limit(8),
            name="taps",
        )(spatial, before, previous, temporal_w, temporal_b.reshape(1, outs), *held)
        column += size
    return decoded[None]


def shards(latent, *rest):
    if lax.axis_size("chan") == 4 and lax.axis_size("frame") % 8 == 0 and latent.shape[0] == 1:
        return split_work(latent, *rest)
    return gathered(latent, *rest)


def solution(mesh):
    placed = (P("frame", "chan", None), P("chan", None), P("chan"), P(None, "chan"), P("chan"))
    return jax.shard_map(
        shards, mesh=mesh, in_specs=placed, out_specs=P("frame", "chan", None), check_vma=False
    )
```
